32 devices in a mesh: gx: 16 (over z, x, core), gy: 2 (over y).
Axes of the slice: x: 2, y: 2, z: 4, core: 2. Of those that a mesh axis runs over, the one named last changes fastest.
Arguments:
- fine_old: float32 [2, 3, 40, 32, 512], P(None, None, None, 'gx', 'gy'), may hold values from -6 to 6
- fine_now: float32 [2, 3, 40, 32, 512], P(None, None, None, 'gx', 'gy'), may hold values from -6 to 6
- coarse_old: float32 [2, 3, 80, 16, 256], P(None, None, None, 'gx', 'gy'), may hold values from -6 to 6
- coarse_now: float32 [2, 3, 80, 16, 256], P(None, None, None, 'gx', 'gy'), may hold values from -6 to 6
- shear_fine: float32 [40, 32, 512], P(None, 'gx', 'gy'), may hold values from 0.3 to 1.2
- lame_fine: float32 [40, 32, 512], P(None, 'gx', 'gy'), may hold values from 0.5 to 2
- shear_coarse: float32 [80, 16, 256], P(None, 'gx', 'gy'), may hold values from 0.3 to 1.2
- lame_coarse: float32 [80, 16, 256], P(None, 'gx', 'gy'), may hold values from 0.5 to 2
- topography: int32 [32, 512], P('gx', 'gy'), may hold values from 0 to 512
Outputs:
- fine_field: float32 [2, 3, 40, 32, 512], P(None, None, None, 'gx', 'gy')
- coarse_field: float32 [2, 3, 80, 16, 256], P(None, None, None, 'gx', 'gy')
- fine_kernel: float32 [40, 32, 512], P(None, 'gx', 'gy')
- coarse_kernel: float32 [80, 16, 256], P(None, 'gx', 'gy')
The draws below stay inside these ranges and needn't reach their ends.
All inputs are finite; a program needn't handle non-finite values.
Results may differ from the reference program's by a relative error of at most 0.0003.
Values sent between devices are 32-bit elements; how exact they have to be, the bound alone decides.
A program may use at most 64 MiB of HBM per device.

```python
import math
import jax
import jax.numpy as jnp
from jax import lax

FZ = 40
CZ = 80
FXD = 2
STEPS = 2
NX = 32
NY = 512
NXC = 16
NYC = 256


def plant(array, key, smallest, high):
    longest = array.shape.index(max(array.shape))
    spots = []
    for shift in (0, 1):
        where = [jax.random.randint(jax.random.fold_in(key, axis), (), 0, length) for axis, length in enumerate(array.shape)]
        where[longest] = (where[longest] + shift) % array.shape[longest]
        spots.append(tuple(where))
    return array.at[spots[0]].set(smallest).at[spots[1]].set(high)


def shard_levels(own_key, dims, split, least, largest):
    factor_of, own = 1.0, jax.random.fold_in(own_key, 6)
    for axis_at, parts in split:
        steps = jnp.exp(jax.random.uniform(jax.random.fold_in(own, axis_at), (parts,), jnp.float32, least / len(split), largest / len(split)))
        factor_of = factor_of * jnp.repeat(steps, dims[axis_at] // parts).reshape([-1 if axis == axis_at else 1 for axis in range(len(dims))])
    return factor_of


def gaussian(rng, extent, scale, reach, cuts=(), kind=jnp.bfloat16):
    array = scale * jax.random.normal(rng, extent, jnp.float32)
    if cuts:
        array = array * shard_levels(rng, extent, cuts, -0.22, 0.18)
    return jnp.clip(array, -reach, reach).astype(kind)


def setup_inputs(seed: int = 0) -> dict:
    keys = jax.random.split(jax.random.key(seed), 10)
    return {
        "fine_old": gaussian(keys[0], (2, 3, FZ, NX, NY), 1.0, 6.0, ((3, 16), (4, 2)), jnp.float32),
        "fine_now": gaussian(keys[1], (2, 3, FZ, NX, NY), 1.0, 6.0, ((3, 16), (4, 2)), jnp.float32),
        "coarse_old": gaussian(keys[2], (2, 3, CZ, NXC, NYC), 1.0, 6.0, ((3, 16), (4, 2)), jnp.float32),
        "coarse_now": gaussian(keys[3], (2, 3, CZ, NXC, NYC), 1.0, 6.0, ((3, 16), (4, 2)), jnp.float32),
        "shear_fine": jnp.clip(jnp.exp(math.log(1.2) - 1.3862944 * jax.random.uniform(keys[4], (FZ, NX, NY), jnp.float32) ** shard_levels(keys[4], (FZ, NX, NY), ((1, 16), (2, 2)), -0.2, 0.2)), 0.3, 1.2),
        "lame_fine": jnp.clip(jnp.exp(math.log(2.0) - 1.3862944 * jax.random.uniform(keys[5], (FZ, NX, NY), jnp.float32) ** shard_levels(keys[5], (FZ, NX, NY), ((1, 16), (2, 2)), -0.2, 0.2)), 0.5, 2.0),
        "shear_coarse": jnp.clip(jnp.exp(math.log(1.2) - 1.3862944 * jax.random.uniform(keys[6], (CZ, NXC, NYC), jnp.float32) ** shard_levels(keys[6], (CZ, NXC, NYC), ((1, 16), (2, 2)), -0.2, 0.2)), 0.3, 1.2),
        "lame_coarse": jnp.clip(jnp.exp(math.log(2.0) - 1.3862944 * jax.random.uniform(keys[7], (CZ, NXC, NYC), jnp.float32) ** shard_levels(keys[7], (CZ, NXC, NYC), ((1, 16), (2, 2)), -0.2, 0.2)), 0.5, 2.0),
        "topography": plant(jax.random.randint(keys[8], (NX, NY), 0, 513), jax.random.fold_in(keys[8], 1), 0, 512).astype(jnp.int32),
    }


STEP_SQUARED = 0.04


def offset(padded, up_down, along_x, along_y):
    depth_cells = padded.shape[2] - 2
    row_count = padded.shape[3] - 2
    column_count = padded.shape[4] - 2
    return padded[:, :, 1 + up_down:1 + up_down + depth_cells, 1 + along_x:1 + along_x + row_count, 1 + along_y:1 + along_y + column_count]


def accelerate(padded, spacing_pad, grid_step, shear, lame):
    center = offset(padded, 0, 0, 0)
    spacing = spacing_pad[1:-1, 1:-1]
    inverse_area = 1.0 / (grid_step * grid_step)
    curve_xx = (offset(padded, 0, 1, 0) - 2.0 * center + offset(padded, 0, -1, 0)) * inverse_area
    curve_yy = (offset(padded, 0, 0, 1) - 2.0 * center + offset(padded, 0, 0, -1)) * inverse_area
    curve_zz = (offset(padded, 1, 0, 0) - 2.0 * center + offset(padded, -1, 0, 0)) / (spacing * spacing)
    mixed_xy = (offset(padded, 0, 1, 1) - offset(padded, 0, 1, -1) - offset(padded, 0, -1, 1) + offset(padded, 0, -1, -1)) * (0.25 * inverse_area)
    east_side = (offset(padded, 1, 1, 0) - offset(padded, -1, 1, 0)) / (2.0 * spacing_pad[2:, 1:-1])
    west_side = (offset(padded, 1, -1, 0) - offset(padded, -1, -1, 0)) / (2.0 * spacing_pad[:-2, 1:-1])
    mixed_xz = (east_side - west_side) * (0.5 / grid_step)
    north_side = (offset(padded, 1, 0, 1) - offset(padded, -1, 0, 1)) / (2.0 * spacing_pad[1:-1, 2:])
    south_side = (offset(padded, 1, 0, -1) - offset(padded, -1, 0, -1)) / (2.0 * spacing_pad[1:-1, :-2])
    mixed_yz = (north_side - south_side) * (0.5 / grid_step)
    laplace = curve_xx + curve_yy + curve_zz
    grad_div = jnp.stack([
        curve_xx[:, 0] + mixed_xy[:, 1] + mixed_xz[:, 2],
        mixed_xy[:, 0] + curve_yy[:, 1] + mixed_yz[:, 2],
        mixed_xz[:, 0] + mixed_yz[:, 1] + curve_zz[:, 2]], axis=1)
    return shear * laplace + (lame + shear) * grad_div


def restrict(plane):
    row_sums = plane[..., 0::2, :] + plane[..., 1::2, :]
    summed = row_sums[..., 0::2] + row_sums[..., 1::2]
    return 0.25 * summed


def prolong(padded_plane):
    middle = 0.75 * padded_plane[..., 1:-1, :]
    even_rows = middle + 0.25 * padded_plane[..., :-2, :]
    odd_rows = middle + 0.25 * padded_plane[..., 2:, :]
    plane_dims = even_rows.shape
    row_pairs = jnp.stack([even_rows, odd_rows], axis=-2).reshape(plane_dims[:-2] + (2 * plane_dims[-2], plane_dims[-1]))
    center_cols = 0.75 * row_pairs[..., 1:-1]
    even_cols = center_cols + 0.25 * row_pairs[..., :-2]
    odd_cols = center_cols + 0.25 * row_pairs[..., 2:]
    col_dims = even_cols.shape
    return jnp.stack([even_cols, odd_cols], axis=-1).reshape(col_dims[:-1] + (2 * col_dims[-1],))


def pad_sides(block):
    return jnp.pad(block, ((0, 0), (0, 0), (0, 0), (1, 1), (1, 1)))


def blocked(padded, spacing_pad, grid_step, shear, lame, block_rows):
    block_count = (padded.shape[3] - 2) // block_rows

    def one_block(block_index):
        first_row = (block_index * block_rows).astype(jnp.int32)
        field_piece = lax.dynamic_slice_in_dim(padded, first_row, block_rows + 2, 3)
        space_piece = lax.dynamic_slice_in_dim(spacing_pad, first_row, block_rows + 2, 0)
        shear_piece = lax.dynamic_slice_in_dim(shear, first_row, block_rows, 1)
        lame_piece = lax.dynamic_slice_in_dim(lame, first_row, block_rows, 1)
        return accelerate(field_piece, space_piece, grid_step, shear_piece, lame_piece)

    pieces = lax.map(one_block, jnp.arange(block_count, dtype=jnp.int32))
    reordered = jnp.moveaxis(pieces, 0, 3)
    dims_now = reordered.shape
    return reordered.reshape(dims_now[:3] + (dims_now[3] * dims_now[4], dims_now[5]))


def reference(fine_old, fine_now, coarse_old, coarse_now, shear_fine, lame_fine, shear_coarse, lame_coarse, topography):
    heights = jnp.pad(topography.astype(jnp.float32), 1)
    fine_space = 1.0 + heights / 1024.0
    coarse_space = jnp.full((NXC + 2, NYC + 2), 2.0, jnp.float32)
    fine_kernel = jnp.zeros((FZ, NX, NY), jnp.float32)
    coarse_kernel = jnp.zeros((CZ, NXC, NYC), jnp.float32)
    for time_level in range(STEPS):
        ridge = restrict(fine_now[:, :, -1])
        floor_plane = jnp.zeros_like(ridge)
        coarse_ext = jnp.concatenate([ridge[:, :, None], coarse_now, floor_plane[:, :, None]], axis=2)
        coarse_pad = pad_sides(coarse_ext)
        ghost = prolong(coarse_pad[:, :, 1])
        fine_ext = jnp.concatenate([fine_now[:, :, :1], fine_now, ghost[:, :, None]], axis=2)
        fine_pad = pad_sides(fine_ext)
        fine_next = 2.0 * fine_now - fine_old + STEP_SQUARED * blocked(fine_pad, fine_space, 1.0, shear_fine, lame_fine, FXD)
        coarse_next = 2.0 * coarse_now - coarse_old + STEP_SQUARED * blocked(coarse_pad, coarse_space, 2.0, shear_coarse, lame_coarse, FXD // 2)
        fine_kernel = fine_kernel + jnp.sum(fine_next[0] * fine_next[1], axis=0)
        coarse_kernel = coarse_kernel + jnp.sum(coarse_next[0] * coarse_next[1], axis=0)
        fine_old, fine_now = fine_now, fine_next
        coarse_old, coarse_now = coarse_now, coarse_next
    return fine_now, coarse_now, fine_kernel, coarse_kernel
```

```python
import functools

import jax
import jax.numpy as jnp
from jax import lax
from jax.experimental import pallas as pl
from jax.experimental.pallas import tpu as pltpu
from jax.sharding import PartitionSpec as P

STEPS = 2
STEP_SQUARED = 0.04
LANES = 128
HALF = LANES // 2
TOP = 8


def stencil(ext, s, depth, own, grid_step, half_inv, inv_sq):
    total = ext.shape[-1]
    inverse_area = 1.0 / (grid_step * grid_step)
    tilt = 0.5 / grid_step

    def rows(slot, c, shift):
        return ext[slot, c, TOP + shift : TOP + shift + depth, :]

    def across(v):
        return pltpu.roll(v, total - 1, 1)[:, :own] - pltpu.roll(v, 1, 1)[:, :own]

    xx, yy, zz, mxy, mxz, myz = [], [], [], {}, {}, {}
    for c in range(3):
        wide = rows(s, c, 0)
        mid = wide[:, :own]
        east, west = rows(s + 1, c, 0), rows(s - 1, c, 0)
        down, up = rows(s, c, 1), rows(s, c, -1)
        twice = 2.0 * mid
        xx.append((east[:, :own] - twice + west[:, :own]) * inverse_area)
        yy.append(
            (pltpu.roll(wide, total - 1, 1)[:, :own] - twice + pltpu.roll(wide, 1, 1)[:, :own])
            * inverse_area
        )
        zz.append((down[:, :own] - twice + up[:, :own]) * inv_sq[s][:, :own])
        if c != 2:
            mxy[c] = across(east - west) * (0.25 * inverse_area)
        if c != 1:
            e = (rows(s + 1, c, 1) - rows(s + 1, c, -1))[:, :own] * half_inv[s + 1][:, :own]
            w = (rows(s - 1, c, 1) - rows(s - 1, c, -1))[:, :own] * half_inv[s - 1][:, :own]
            mxz[c] = (e - w) * tilt
        if c != 0:
            myz[c] = across((down - up) * half_inv[s]) * tilt
    laplace = [xx[c] + yy[c] + zz[c] for c in range(3)]
    grad_div = [
        xx[0] + mxy[1] + mxz[2],
        mxy[0] + yy[1] + myz[2],
        mxz[0] + myz[1] + zz[2],
    ]
    return laplace, grad_div


def body(
    nx, ny, fz, cz, fy, cy,
    fold, fnow, cold, cnow, shf, laf, shc, lac, topo,
    fout, cout, fker, cker,
    fn, cn, xf, xc, xg, pk, yr, mg, jown, jx, ext, extc, ghin, ghost,
    xs, xr, gs, gr, ys, yrs, js, jr,
):
    gx, gy = lax.axis_index("gx"), lax.axis_index("gy")
    has_x = (gx > 0, gx < nx - 1)
    has_y = (gy > 0, gy < ny - 1)
    tiles = fy // LANES
    rows_c = cn.shape[2]

    barrier = pltpu.get_barrier_semaphore()
    for side in range(2):
        step = 2 * side - 1

        @pl.when(has_x[side])
        def _():
            pl.semaphore_signal(barrier, inc=1, device_id={"gx": gx + step})

        @pl.when(has_y[side])
        def _():
            pl.semaphore_signal(barrier, inc=1, device_id={"gy": gy + step})

        @pl.when(jnp.logical_not(has_x[side]))
        def _():
            xf[:, side] = jnp.zeros(xf.shape[:1] + xf.shape[2:], jnp.float32)
            xc[:, side] = jnp.zeros(xc.shape[:1] + xc.shape[2:], jnp.float32)
            xg[:, side] = jnp.zeros(xg.shape[:1] + xg.shape[2:], jnp.float32)
            jx[side] = jnp.ones(jx.shape[1:], jnp.float32)

        @pl.when(jnp.logical_not(has_y[side]))
        def _():
            yr[:, side] = jnp.zeros(yr.shape[:1] + yr.shape[2:], jnp.float32)

    def x_copies(t, f, d):
        part = pl.ds(3 * f, 3)
        dev = {"gx": gx + 2 * d - 1}
        return (
            pltpu.make_async_remote_copy(
                cn.at[t, part], xc.at[t, 1 - d, part], xs.at[t, d, f, 0], xr.at[t, 1 - d, f, 0],
                device_id=dev,
            ),
            pltpu.make_async_remote_copy(
                fn.at[t, d, part], xf.at[t, 1 - d, part], xs.at[t, d, f, 1], xr.at[t, 1 - d, f, 1],
                device_id=dev,
            ),
        )

    def x_wait_copies(t, f, d):
        part = pl.ds(3 * f, 3)
        dev = {"gx": gx + 2 * d - 1}
        return (
            pltpu.make_async_remote_copy(
                cn.at[t, part], xc.at[t, d, part], xs.at[t, d, f, 0], xr.at[t, d, f, 0],
                device_id=dev,
            ),
            pltpu.make_async_remote_copy(
                fn.at[t, d, part], xf.at[t, d, part], xs.at[t, d, f, 1], xr.at[t, d, f, 1],
                device_id=dev,
            ),
        )

    def g_copy(t, d, land):
        return pltpu.make_async_remote_copy(
            mg.at[t], xg.at[t, land], gs.at[t, d], gr.at[t, land], device_id={"gx": gx + 2 * d - 1}
        )

    def y_copy(t, d, land):
        return pltpu.make_async_remote_copy(
            pk.at[t, d], yr.at[t, land], ys.at[t, d], yrs.at[t, land],
            device_id={"gy": gy + 2 * d - 1},
        )

    def j_copy(d, land):
        return pltpu.make_async_remote_copy(
            jown, jx.at[land], js.at[d], jr.at[land], device_id={"gx": gx + 2 * d - 1}
        )

    def each(flags, action):
        for d in range(2):
            pl.when(flags[d])(functools.partial(action, d))

    def send_x(t, f):
        def go(d):
            for copy in x_copies(t, f, d):
                copy.start()

        each(has_x, go)

    lane_f = lax.broadcasted_iota(jnp.int32, (fz, LANES), 1)
    lane_c = lax.broadcasted_iota(jnp.int32, (rows_c, LANES), 1)

    pair_row = lax.broadcasted_iota(jnp.int32, (fy, cy), 0)
    pair_col = lax.broadcasted_iota(jnp.int32, (fy, cy), 1)
    pairs = jnp.where(pair_row // 2 == pair_col, 0.25, 0.0).astype(jnp.float32)
    src = lax.broadcasted_iota(jnp.int32, (cy + LANES, fy + LANES), 0)
    dst = lax.broadcasted_iota(jnp.int32, (cy + LANES, fy + LANES), 1)
    src = jnp.where(src == cy + LANES - 1, -1, src)
    dst = jnp.where(dst == fy + LANES - 1, -1, dst)
    near = (dst + 2) // 2 - 1
    other = near + 2 * (dst + 2 - 2 * (near + 1)) - 1
    spread = jnp.where(src == near, 0.75, jnp.where(src == other, 0.25, 0.0)).astype(jnp.float32)

    def dot(a, b):
        return lax.dot_general(
            a, b, (((1,), (0,)), ((), ())),
            precision=lax.Precision.HIGHEST, preferred_element_type=jnp.float32,
        )

    def set_ridge(t, f):
        ghin[...] = jnp.zeros(ghin.shape, jnp.float32)
        for c in range(3):
            i = 3 * f + c
            ghin[c : c + 1, :fy] = fn[t, 0, i, fz - 1 : fz, :] + fn[t, 1, i, fz - 1 : fz, :]
        ridge = dot(ghin[0:8, :fy], pairs)
        for c in range(3):
            cn[t, 3 * f + c, cz : cz + 8, :] = jnp.broadcast_to(ridge[c : c + 1], (8, cy))

    jown[...] = jnp.ones(jown.shape, jnp.float32)
    jown[0:2, :] = 1.0 + topo[...].astype(jnp.float32) * (1.0 / 1024.0)
    for f in range(2):
        for i in range(3 * f, 3 * f + 3):
            cn[0, i, 0:cz, :] = cnow[i]
            for x in range(2):
                for y in range(tiles):
                    fn[0, x, i, :, y * LANES : (y + 1) * LANES] = fnow[
                        i, pl.ds(2 * y + x, fz, stride=2 * tiles), :
                    ]
        set_ridge(0, f)
    count = sum(h.astype(jnp.int32) for h in has_x + has_y)
    pl.semaphore_wait(barrier, count)
    each(has_x, lambda d: j_copy(d, 1 - d).start())
    send_x(0, 0)

    def pack(t):
        for d in range(2):
            base = HALF * (1 - d)
            at = (0, fy - 1)[d]
            fine = jnp.zeros((fz, LANES), jnp.float32)
            for i in range(6):
                for x in range(2):
                    fine = jnp.where(lane_f == base + 2 * i + x, fn[t, x, i, :, at : at + 1], fine)
            if t == 0:
                for x in range(2):
                    fine = jnp.where(
                        lane_f == base + 12 + x, jown[x : x + 1, at : at + 1], fine
                    )
            coarse = jnp.zeros((rows_c, LANES), jnp.float32)
            at = (0, cy - 1)[d]
            for i in range(6):
                coarse = jnp.where(lane_c == base + i, cn[t, i, :, at : at + 1], coarse)
            pk[t, d, 0:fz, :] = fine
            pk[t, d, fz : fz + rows_c, :] = coarse

    def exchange_columns(t):
        pack(t)
        each(has_y, lambda d: y_copy(t, d, 1 - d).start())
        each(has_y, lambda d: y_copy(t, d, d).wait_recv())
        low = lax.broadcasted_iota(jnp.int32, mg.shape[1:], 1) < HALF
        mg[t] = jnp.where(low, yr[t, 0], yr[t, 1])
        each(has_x, lambda d: g_copy(t, d, 1 - d).start())

    exchange_columns(0)
    send_x(0, 1)

    def halo_tile(v, k, lane):
        return jnp.where(
            lane == 0,
            v[:, HALF + k : HALF + k + 1],
            jnp.where(lane == LANES - 1, v[:, k : k + 1], 0.0),
        )

    each(has_x, lambda d: j_copy(d, d).wait_recv())
    lane_1 = lax.broadcasted_iota(jnp.int32, (1, LANES), 1)
    half_inv, inv_sq = {}, {}
    for q in range(4):
        if q in (0, 3):
            row = jx[0, 1:2, :] if q == 0 else jx[1, 0:1, :]
            edge = jnp.ones((1, LANES), jnp.float32)
        else:
            row = jown[q - 1 : q, :]
            head = mg[0, 0:8, :][0:1]
            edge = halo_tile(head, 12 + q - 1, lane_1)
            edge = jnp.where(edge == 0.0, 1.0, edge)
        row = jnp.concatenate([row, edge], axis=1)
        half_inv[q] = 0.5 / row
        inv_sq[q] = 1.0 / (row * row)
    half_c = {q: jnp.full((1, cy + LANES), 0.25, jnp.float32) for q in range(3)}
    sq_c = {q: jnp.full((1, cy + LANES), 0.25, jnp.float32) for q in range(3)}

    lane_g = lax.broadcasted_iota(jnp.int32, (16, fy + LANES), 1)
    row_g = lax.broadcasted_iota(jnp.int32, (16, fy + LANES), 0)
    keep = (lane_g < fy)
    keep = keep | ((lane_g == fy) & has_y[1]) | ((lane_g == fy + LANES - 1) & has_y[0])
    keep = keep & ((row_g >= 3) | has_x[0]) & ((row_g < 9) | has_x[1])

    for t in range(STEPS):
        for f in range(2):
            if t > 0 and f == 0:
                exchange_columns(t)
                send_x(t, 1)

            def coarse_in(d):
                x_wait_copies(t, f, d)[0].wait_recv()
                if f == 0:
                    g_copy(t, d, d).wait_recv()

            each(has_x, coarse_in)
            for q in range(3):
                cols = mg.at[t] if q == 1 else xg.at[t, q // 2]
                cols = cols[fz : fz + rows_c, :]
                for c in range(3):
                    i = 3 * f + c
                    plane = cn[t, i] if q == 1 else xc[t, q // 2, i]
                    whole = jnp.concatenate([plane, halo_tile(cols, i, lane_c)], axis=1)
                    extc[q, c, TOP : TOP + cz, :] = whole[0:cz]
                    extc[q, c, TOP - 1 : TOP, :] = whole[cz : cz + 1]
                    extc[q, c, TOP + cz : TOP + cz + 1, :] = jnp.zeros((1, cy + LANES), jnp.float32)
            laplace, grad_div = stencil(extc, 1, cz, cy, 2.0, half_c, sq_c)
            for c in range(3):
                i = 3 * f + c
                before = cold[i] if t == 0 else cn[t - 1, i, 0:cz, :]
                mu = shc[...]
                new = 2.0 * cn[t, i, 0:cz, :] - before + STEP_SQUARED * (
                    mu * laplace[c] + (lac[...] + mu) * grad_div[c]
                )
                if t < STEPS - 1:
                    cn[t + 1, i, 0:cz, :] = new
                else:
                    cout[i] = new

            ghin[...] = jnp.zeros(ghin.shape, jnp.float32)
            for c in range(3):
                low, mid, high = (extc[q, c, TOP : TOP + 1, :] for q in range(3))
                quads = (
                    0.75 * low + 0.25 * mid,
                    0.75 * mid + 0.25 * low,
                    0.75 * mid + 0.25 * high,
                    0.75 * high + 0.25 * mid,
                )
                for q in range(4):
                    ghin[3 * q + c : 3 * q + c + 1, : cy + LANES] = quads[q]
            ghost[...] = jnp.where(keep, dot(ghin[:, : cy + LANES], spread), 0.0)

            each(has_x, lambda d: x_wait_copies(t, f, d)[1].wait_recv())
            for q in range(4):
                cols = xg[t, q // 3, 0:fz, :] if q in (0, 3) else mg[t, 0:fz, :]
                x = (1, 0, 1, 0)[q]
                for c in range(3):
                    i = 3 * f + c
                    plane = xf[t, q // 3, i] if q in (0, 3) else fn[t, x, i]
                    whole = jnp.concatenate([plane, halo_tile(cols, 2 * i + x, lane_f)], axis=1)
                    ext[q, c, TOP : TOP + fz, :] = whole
                    ext[q, c, TOP - 1 : TOP, :] = whole[0:1]
                    ext[q, c, TOP + fz : TOP + fz + 1, :] = ghost[3 * q + c : 3 * q + c + 1, :]
            for x in range(2):
                laplace, grad_div = stencil(ext, x + 1, fz, fy, 1.0, half_inv, inv_sq)
                picks = [pl.ds(2 * y + x, fz, stride=2 * tiles) for y in range(tiles)]

                def fetch(*at):
                    return jnp.concatenate([at[0][at[1:] + (p, slice(None))] for p in picks], axis=1)

                mu = fetch(shf)
                both = fetch(laf) + mu
                for c in range(3):
                    i = 3 * f + c
                    before = fetch(fold, i) if t == 0 else fn[t - 1, x, i]
                    new = 2.0 * fn[t, x, i] - before + STEP_SQUARED * (
                        mu * laplace[c] + both * grad_div[c]
                    )
                    fn[t + 1, x, i] = new
                    if t == STEPS - 1:
                        for y in range(tiles):
                            fout[i, picks[y], :] = new[:, y * LANES : (y + 1) * LANES]
            if t < STEPS - 1:
                set_ridge(t + 1, f)
                if f == 0:
                    send_x(t + 1, 0)

        def later(i):
            return cn[t + 1, i, 0:cz, :] if t < STEPS - 1 else cout[i]

        prod = later(0) * later(3) + later(1) * later(4) + later(2) * later(5)
        cker[...] = prod if t == 0 else cker[...] + prod
        for x in range(2):
            prod = sum(fn[t + 1, x, c] * fn[t + 1, x, c + 3] for c in range(3))
            for y in range(tiles):
                piece = prod[:, y * LANES : (y + 1) * LANES]
                pick = pl.ds(2 * y + x, fz, stride=2 * tiles)
                fker[pick, :] = piece if t == 0 else fker[pick, :] + piece

    def finish_x(d):
        j_copy(d, d).wait_send()
        for t in range(STEPS):
            g_copy(t, d, d).wait_send()
            for f in range(2):
                for copy in x_wait_copies(t, f, d):
                    copy.wait_send()

    def finish_y(d):
        for t in range(STEPS):
            y_copy(t, d, d).wait_send()

    each(has_x, finish_x)
    each(has_y, finish_y)


def rows_view(a):
    lead = a.shape[:-3]
    fz, fx, fy = a.shape[-3:]
    n = len(lead)
    a = a.reshape(lead + (fz, fx, fy // LANES, LANES))
    a = a.transpose(tuple(range(n)) + (n, n + 2, n + 1, n + 3))
    return a.reshape(((6,) if lead else ()) + (fz * fx * fy // LANES, LANES))


def rows_back(a, shape):
    lead = shape[:-3]
    fz, fx, fy = shape[-3:]
    n = len(lead)
    a = a.reshape(lead + (fz, fy // LANES, fx, LANES))
    a = a.transpose(tuple(range(n)) + (n, n + 2, n + 1, n + 3))
    return a.reshape(shape)


def on_device(fold, fnow, cold, cnow, shf, laf, shc, lac, topo):
    nx, ny = lax.axis_size("gx"), lax.axis_size("gy")
    fz, fx, fy = shf.shape
    cz, cx, cy = shc.shape
    if fx != 2 or cx != 1 or cy != LANES or fy != 2 * cy:
        raise ValueError("unsupported tile")
    rows_c = cz + 8
    f32 = jnp.float32
    dma = pltpu.SemaphoreType.DMA
    nrows = fz * fx * fy // LANES
    vm = pl.BlockSpec(memory_space=pltpu.VMEM)
    fout, cout, fker, cker = pl.pallas_call(
        functools.partial(body, nx, ny, fz, cz, fy, cy),
        out_shape=(
            jax.ShapeDtypeStruct((6, nrows, LANES), f32),
            jax.ShapeDtypeStruct((6, cz, cy), f32),
            jax.ShapeDtypeStruct((nrows, LANES), f32),
            jax.ShapeDtypeStruct((cz, cy), f32),
        ),
        in_specs=[vm] * 9,
        out_specs=(vm,) * 4,
        scratch_shapes=[
            pltpu.VMEM((STEPS + 1, 2, 6, fz, fy), f32),
            pltpu.VMEM((STEPS, 6, rows_c, cy), f32),
            pltpu.VMEM((STEPS, 2, 6, fz, fy), f32),
            pltpu.VMEM((STEPS, 2, 6, rows_c, cy), f32),
            pltpu.VMEM((STEPS, 2, fz + rows_c, LANES), f32),
            pltpu.VMEM((STEPS, 2, fz + rows_c, LANES), f32),
            pltpu.VMEM((STEPS, 2, fz + rows_c, LANES), f32),
            pltpu.VMEM((STEPS, fz + rows_c, LANES), f32),
            pltpu.VMEM((8, fy), f32),
            pltpu.VMEM((2, 8, fy), f32),
            pltpu.VMEM((4, 3, fz + 16, fy + LANES), f32),
            pltpu.VMEM((3, 3, cz + 16, cy + LANES), f32),
            pltpu.VMEM((16, max(fy, cy + LANES)), f32),
            pltpu.VMEM((16, fy + LANES), f32),
            dma((STEPS, 2, 2, 2)),
            dma((STEPS, 2, 2, 2)),
            dma((STEPS, 2)),
            dma((STEPS, 2)),
            dma((STEPS, 2)),
            dma((STEPS, 2)),
            dma((2,)),
            dma((2,)),
        ],
        compiler_params=pltpu.CompilerParams(collective_id=0, has_side_effects=True),
        name="wave",
    )(
        rows_view(fold),
        rows_view(fnow),
        cold.reshape(6, cz, cy),
        cnow.reshape(6, cz, cy),
        rows_view(shf),
        rows_view(laf),
        shc.reshape(cz, cy),
        lac.reshape(cz, cy),
        topo,
    )
    return (
        rows_back(fout, fold.shape),
        cout.reshape(cold.shape),
        rows_back(fker, shf.shape),
        cker.reshape(shc.shape),
    )


def solution(mesh):
    field, coef = P(None, None, None, "gx", "gy"), P(None, "gx", "gy")
    return jax.shard_map(
        on_device,
        mesh=mesh,
        in_specs=(field,) * 4 + (coef,) * 4 + (P("gx", "gy"),),
        out_specs=(field, field, coef, coef),
        check_vma=False,
    )
```

```python
import functools

import jax
import jax.numpy as jnp
from jax import lax
from jax.experimental import pallas as pl
from jax.experimental.pallas import tpu as pltpu
from jax.sharding import PartitionSpec as P

STEPS = 2
STEP_SQUARED = 0.04
LANES = 128
HALF = LANES // 2
TOP = 8
FIRST, SECOND = 16, 24


def stencil(ext, s, depth, own, grid_step, half_inv, inv_sq):
    total = ext.shape[-1]
    inverse_area = 1.0 / (grid_step * grid_step)
    tilt = 0.5 / grid_step

    def rows(slot, c, shift):
        return ext[slot, c, TOP + shift : TOP + shift + depth, :]

    def across(v):
        return pltpu.roll(v, total - 1, 1)[:, :own] - pltpu.roll(v, 1, 1)[:, :own]

    xx, yy, zz, mxy, mxz, myz = [], [], [], {}, {}, {}
    for c in range(3):
        wide = rows(s, c, 0)
        mid = wide[:, :own]
        east, west = rows(s + 1, c, 0), rows(s - 1, c, 0)
        down, up = rows(s, c, 1), rows(s, c, -1)
        twice = 2.0 * mid
        xx.append((east[:, :own] - twice + west[:, :own]) * inverse_area)
        yy.append(
            (pltpu.roll(wide, total - 1, 1)[:, :own] - twice + pltpu.roll(wide, 1, 1)[:, :own])
            * inverse_area
        )
        zz.append((down[:, :own] - twice + up[:, :own]) * inv_sq[s][:, :own])
        if c != 2:
            mxy[c] = across(east - west) * (0.25 * inverse_area)
        if c != 1:
            e = (rows(s + 1, c, 1) - rows(s + 1, c, -1))[:, :own] * half_inv[s + 1][:, :own]
            w = (rows(s - 1, c, 1) - rows(s - 1, c, -1))[:, :own] * half_inv[s - 1][:, :own]
            mxz[c] = (e - w) * tilt
        if c != 0:
            myz[c] = across((down - up) * half_inv[s]) * tilt
    laplace = [xx[c] + yy[c] + zz[c] for c in range(3)]
    grad_div = [
        xx[0] + mxy[1] + mxz[2],
        mxy[0] + yy[1] + myz[2],
        mxz[0] + myz[1] + zz[2],
    ]
    return laplace, grad_div


def body(
    nx, ny, fz, cz, fy, cy,
    fold, fnow, cold, cnow, shf, laf, shc, lac, topo,
    fout, cout, fker, cker,
    fn, cn, xf, xc, xg, pk, yr, mg, jown, jx, ext, extc, ghin, ghost,
    xs, xr, gs, gr, ys, yrs, js, jr,
):
    gx, gy = lax.axis_index("gx"), lax.axis_index("gy")
    has_x = (gx > 0, gx < nx - 1)
    has_y = (gy > 0, gy < ny - 1)
    tiles = fy // LANES
    rows_c = cn.shape[2]
    split = mg.shape[1]

    barrier = pltpu.get_barrier_semaphore()
    for side in range(2):
        step = 2 * side - 1

        @pl.when(has_x[side])
        def _():
            pl.semaphore_signal(barrier, inc=1, device_id={"gx": gx + step})

        @pl.when(has_y[side])
        def _():
            pl.semaphore_signal(barrier, inc=1, device_id={"gy": gy + step})

        @pl.when(jnp.logical_not(has_x[side]))
        def _():
            xf[:, side] = jnp.zeros(xf.shape[:1] + xf.shape[2:], jnp.float32)
            xc[:, side] = jnp.zeros(xc.shape[:1] + xc.shape[2:], jnp.float32)
            xg[:, side] = jnp.zeros(xg.shape[:1] + xg.shape[2:], jnp.float32)
            jx[side] = jnp.ones(jx.shape[1:], jnp.float32)

        @pl.when(jnp.logical_not(has_y[side]))
        def _():
            yr[:, side] = jnp.zeros(yr.shape[:1] + yr.shape[2:], jnp.float32)

    def x_copies(t, f, d):
        part = pl.ds(3 * f, 3)
        dev = {"gx": gx + 2 * d - 1}
        return (
            pltpu.make_async_remote_copy(
                cn.at[t, part], xc.at[t, 1 - d, part], xs.at[t, d, f, 0], xr.at[t, 1 - d, f, 0],
                device_id=dev,
            ),
            pltpu.make_async_remote_copy(
                fn.at[t, d, part], xf.at[t, 1 - d, part], xs.at[t, d, f, 1], xr.at[t, 1 - d, f, 1],
                device_id=dev,
            ),
        )

    def x_wait_copies(t, f, d):
        part = pl.ds(3 * f, 3)
        dev = {"gx": gx + 2 * d - 1}
        return (
            pltpu.make_async_remote_copy(
                cn.at[t, part], xc.at[t, d, part], xs.at[t, d, f, 0], xr.at[t, d, f, 0],
                device_id=dev,
            ),
            pltpu.make_async_remote_copy(
                fn.at[t, d, part], xf.at[t, d, part], xs.at[t, d, f, 1], xr.at[t, d, f, 1],
                device_id=dev,
            ),
        )

    def g_copy(t, d, land):
        return pltpu.make_async_remote_copy(
            mg.at[t], xg.at[t, land], gs.at[t, d], gr.at[t, land], device_id={"gx": gx + 2 * d - 1}
        )

    def y_copy(t, d, land):
        return pltpu.make_async_remote_copy(
            pk.at[t, d], yr.at[t, land], ys.at[t, d], yrs.at[t, land],
            device_id={"gy": gy + 2 * d - 1},
        )

    def j_copy(d, land):
        return pltpu.make_async_remote_copy(
            jown, jx.at[land], js.at[d], jr.at[land], device_id={"gx": gx + 2 * d - 1}
        )

    def each(flags, action):
        for d in range(2):
            pl.when(flags[d])(functools.partial(action, d))

    def send_x(t, f):
        def go(d):
            for copy in x_copies(t, f, d):
                copy.start()

        each(has_x, go)

    lane_f = lax.broadcasted_iota(jnp.int32, (fz, LANES), 1)
    lane_c = lax.broadcasted_iota(jnp.int32, (rows_c, LANES), 1)

    pair_row = lax.broadcasted_iota(jnp.int32, (fy, cy), 0)
    pair_col = lax.broadcasted_iota(jnp.int32, (fy, cy), 1)
    pairs = jnp.where(pair_row // 2 == pair_col, 0.25, 0.0).astype(jnp.float32)
    src = lax.broadcasted_iota(jnp.int32, (cy + LANES, fy + LANES), 0)
    dst = lax.broadcasted_iota(jnp.int32, (cy + LANES, fy + LANES), 1)
    src = jnp.where(src == cy + LANES - 1, -1, src)
    dst = jnp.where(dst == fy + LANES - 1, -1, dst)
    near = (dst + 2) // 2 - 1
    other = near + 2 * (dst + 2 - 2 * (near + 1)) - 1
    spread = jnp.where(src == near, 0.75, jnp.where(src == other, 0.25, 0.0)).astype(jnp.float32)

    def dot(a, b):
        return lax.dot_general(
            a, b, (((1,), (0,)), ((), ())),
            precision=lax.Precision.HIGHEST, preferred_element_type=jnp.float32,
        )

    def set_ridge(t, f):
        ghin[...] = jnp.zeros(ghin.shape, jnp.float32)
        for c in range(3):
            i = 3 * f + c
            ghin[c : c + 1, :fy] = fn[t, 0, i, fz - 1 : fz, :] + fn[t, 1, i, fz - 1 : fz, :]
        ridge = dot(ghin[0:8, :fy], pairs)
        for c in range(3):
            cn[t, 3 * f + c, cz : cz + 8, :] = jnp.broadcast_to(ridge[c : c + 1], (8, cy))

    jown[...] = jnp.ones(jown.shape, jnp.float32)
    jown[0:2, :] = 1.0 + topo[...].astype(jnp.float32) * (1.0 / 1024.0)
    for f in range(2):
        for i in range(3 * f, 3 * f + 3):
            cn[0, i, 0:cz, :] = cnow[i]
            for x in range(2):
                for y in range(tiles):
                    fn[0, x, i, :, y * LANES : (y + 1) * LANES] = fnow[
                        i, pl.ds(2 * y + x, fz, stride=2 * tiles), :
                    ]
        set_ridge(0, f)
    count = sum(h.astype(jnp.int32) for h in has_x + has_y)
    pl.semaphore_wait(barrier, count)
    each(has_x, lambda d: j_copy(d, 1 - d).start())
    send_x(0, 0)

    def pack(t):
        for d in range(2):
            base = HALF * (1 - d)
            at = (0, fy - 1)[d]
            fine = jnp.zeros((fz, LANES), jnp.float32)
            for i in range(6):
                for x in range(2):
                    fine = jnp.where(lane_f == base + 2 * i + x, fn[t, x, i, :, at : at + 1], fine)
            if t == 0:
                for x in range(2):
                    fine = jnp.where(
                        lane_f == base + 12 + x, jown[x : x + 1, at : at + 1], fine
                    )
            coarse = jnp.zeros((rows_c, LANES), jnp.float32)
            at = (0, cy - 1)[d]
            for i in range(6):
                column = cn[t, i, :, at : at + 1]
                coarse = jnp.where(lane_c == base + FIRST + i, column, coarse)
                coarse = jnp.where(lane_c == base + SECOND + i, column, coarse)
            upper = lax.broadcasted_iota(jnp.int32, (split, LANES), 1) % HALF < SECOND
            bottom = jnp.concatenate(
                [coarse[split:], jnp.zeros((2 * split - rows_c, LANES), jnp.float32)], axis=0
            )
            top = jnp.concatenate([fine, jnp.zeros((split - fz, LANES), jnp.float32)], axis=0)
            pk[t, d] = top + jnp.where(upper, coarse[0:split], bottom)

    def exchange_columns(t):
        pack(t)
        each(has_y, lambda d: y_copy(t, d, 1 - d).start())
        each(has_y, lambda d: y_copy(t, d, d).wait_recv())
        low = lax.broadcasted_iota(jnp.int32, mg.shape[1:], 1) < HALF
        mg[t] = jnp.where(low, yr[t, 0], yr[t, 1])
        each(has_x, lambda d: g_copy(t, d, 1 - d).start())

    exchange_columns(0)
    send_x(0, 1)

    def halo_tile(v, k, lane):
        return jnp.where(
            lane == 0,
            v[:, HALF + k : HALF + k + 1],
            jnp.where(lane == LANES - 1, v[:, k : k + 1], 0.0),
        )

    lane_s = lax.broadcasted_iota(jnp.int32, (split, LANES), 1)

    def coarse_tile(v, i):
        first, second = halo_tile(v, FIRST + i, lane_s), halo_tile(v, SECOND + i, lane_s)
        return jnp.concatenate([first, second[: rows_c - split]], axis=0)

    each(has_x, lambda d: j_copy(d, d).wait_recv())
    lane_1 = lax.broadcasted_iota(jnp.int32, (1, LANES), 1)
    half_inv, inv_sq = {}, {}
    for q in range(4):
        if q in (0, 3):
            row = jx[0, 1:2, :] if q == 0 else jx[1, 0:1, :]
            edge = jnp.ones((1, LANES), jnp.float32)
        else:
            row = jown[q - 1 : q, :]
            head = mg[0, 0:8, :][0:1]
            edge = halo_tile(head, 12 + q - 1, lane_1)
            edge = jnp.where(edge == 0.0, 1.0, edge)
        row = jnp.concatenate([row, edge], axis=1)
        half_inv[q] = 0.5 / row
        inv_sq[q] = 1.0 / (row * row)
    half_c = {q: jnp.full((1, cy + LANES), 0.25, jnp.float32) for q in range(3)}
    sq_c = {q: jnp.full((1, cy + LANES), 0.25, jnp.float32) for q in range(3)}

    lane_g = lax.broadcasted_iota(jnp.int32, (16, fy + LANES), 1)
    row_g = lax.broadcasted_iota(jnp.int32, (16, fy + LANES), 0)
    keep = (lane_g < fy)
    keep = keep | ((lane_g == fy) & has_y[1]) | ((lane_g == fy + LANES - 1) & has_y[0])
    keep = keep & ((row_g >= 3) | has_x[0]) & ((row_g < 9) | has_x[1])

    for t in range(STEPS):
        for f in range(2):
            if t > 0 and f == 0:
                exchange_columns(t)
                send_x(t, 1)

            def coarse_in(d):
                x_wait_copies(t, f, d)[0].wait_recv()
                if f == 0:
                    g_copy(t, d, d).wait_recv()

            each(has_x, coarse_in)
            for q in range(3):
                cols = mg.at[t] if q == 1 else xg.at[t, q // 2]
                cols = cols[...]
                for c in range(3):
                    i = 3 * f + c
                    plane = cn[t, i] if q == 1 else xc[t, q // 2, i]
                    whole = jnp.concatenate([plane, coarse_tile(cols, i)], axis=1)
                    extc[q, c, TOP : TOP + cz, :] = whole[0:cz]
                    extc[q, c, TOP - 1 : TOP, :] = whole[cz : cz + 1]
                    extc[q, c, TOP + cz : TOP + cz + 1, :] = jnp.zeros((1, cy + LANES), jnp.float32)
            laplace, grad_div = stencil(extc, 1, cz, cy, 2.0, half_c, sq_c)
            for c in range(3):
                i = 3 * f + c
                before = cold[i] if t == 0 else cn[t - 1, i, 0:cz, :]
                mu = shc[...]
                new = 2.0 * cn[t, i, 0:cz, :] - before + STEP_SQUARED * (
                    mu * laplace[c] + (lac[...] + mu) * grad_div[c]
                )
                if t < STEPS - 1:
                    cn[t + 1, i, 0:cz, :] = new
                else:
                    cout[i] = new

            ghin[...] = jnp.zeros(ghin.shape, jnp.float32)
            for c in range(3):
                low, mid, high = (extc[q, c, TOP : TOP + 1, :] for q in range(3))
                quads = (
                    0.75 * low + 0.25 * mid,
                    0.75 * mid + 0.25 * low,
                    0.75 * mid + 0.25 * high,
                    0.75 * high + 0.25 * mid,
                )
                for q in range(4):
                    ghin[3 * q + c : 3 * q + c + 1, : cy + LANES] = quads[q]
            ghost[...] = jnp.where(keep, dot(ghin[:, : cy + LANES], spread), 0.0)

            each(has_x, lambda d: x_wait_copies(t, f, d)[1].wait_recv())
            for q in range(4):
                cols = xg[t, q // 3, 0:fz, :] if q in (0, 3) else mg[t, 0:fz, :]
                x = (1, 0, 1, 0)[q]
                for c in range(3):
                    i = 3 * f + c
                    plane = xf[t, q // 3, i] if q in (0, 3) else fn[t, x, i]
                    whole = jnp.concatenate([plane, halo_tile(cols, 2 * i + x, lane_f)], axis=1)
                    ext[q, c, TOP : TOP + fz, :] = whole
                    ext[q, c, TOP - 1 : TOP, :] = whole[0:1]
                    ext[q, c, TOP + fz : TOP + fz + 1, :] = ghost[3 * q + c : 3 * q + c + 1, :]
            for x in range(2):
                laplace, grad_div = stencil(ext, x + 1, fz, fy, 1.0, half_inv, inv_sq)
                picks = [pl.ds(2 * y + x, fz, stride=2 * tiles) for y in range(tiles)]

                def fetch(*at):
                    return jnp.concatenate([at[0][at[1:] + (p, slice(None))] for p in picks], axis=1)

                mu = fetch(shf)
                both = fetch(laf) + mu
                for c in range(3):
                    i = 3 * f + c
                    before = fetch(fold, i) if t == 0 else fn[t - 1, x, i]
                    new = 2.0 * fn[t, x, i] - before + STEP_SQUARED * (
                        mu * laplace[c] + both * grad_div[c]
                    )
                    fn[t + 1, x, i] = new
                    if t == STEPS - 1:
                        for y in range(tiles):
                            fout[i, picks[y], :] = new[:, y * LANES : (y + 1) * LANES]
            if t < STEPS - 1:
                set_ridge(t + 1, f)
                if f == 0:
                    send_x(t + 1, 0)

        def later(i):
            return cn[t + 1, i, 0:cz, :] if t < STEPS - 1 else cout[i]

        prod = later(0) * later(3) + later(1) * later(4) + later(2) * later(5)
        cker[...] = prod if t == 0 else cker[...] + prod
        for x in range(2):
            prod = sum(fn[t + 1, x, c] * fn[t + 1, x, c + 3] for c in range(3))
            for y in range(tiles):
                piece = prod[:, y * LANES : (y + 1) * LANES]
                pick = pl.ds(2 * y + x, fz, stride=2 * tiles)
                fker[pick, :] = piece if t == 0 else fker[pick, :] + piece

    def finish_x(d):
        j_copy(d, d).wait_send()
        for t in range(STEPS):
            g_copy(t, d, d).wait_send()
            for f in range(2):
                for copy in x_wait_copies(t, f, d):
                    copy.wait_send()

    def finish_y(d):
        for t in range(STEPS):
            y_copy(t, d, d).wait_send()

    each(has_x, finish_x)
    each(has_y, finish_y)


def rows_view(a):
    lead = a.shape[:-3]
    fz, fx, fy = a.shape[-3:]
    n = len(lead)
    a = a.reshape(lead + (fz, fx, fy // LANES, LANES))
    a = a.transpose(tuple(range(n)) + (n, n + 2, n + 1, n + 3))
    return a.reshape(((6,) if lead else ()) + (fz * fx * fy // LANES, LANES))


def rows_back(a, shape):
    lead = shape[:-3]
    fz, fx, fy = shape[-3:]
    n = len(lead)
    a = a.reshape(lead + (fz, fy // LANES, fx, LANES))
    a = a.transpose(tuple(range(n)) + (n, n + 2, n + 1, n + 3))
    return a.reshape(shape)


def on_device(fold, fnow, cold, cnow, shf, laf, shc, lac, topo):
    nx, ny = lax.axis_size("gx"), lax.axis_size("gy")
    fz, fx, fy = shf.shape
    cz, cx, cy = shc.shape
    if fx != 2 or cx != 1 or cy != LANES or fy != 2 * cy:
        raise ValueError("unsupported tile")
    rows_c = cz + 8
    split = 8 * max(pl.cdiv(fz, 8), pl.cdiv(rows_c, 16))
    f32 = jnp.float32
    dma = pltpu.SemaphoreType.DMA
    nrows = fz * fx * fy // LANES
    vm = pl.BlockSpec(memory_space=pltpu.VMEM)
    fout, cout, fker, cker = pl.pallas_call(
        functools.partial(body, nx, ny, fz, cz, fy, cy),
        out_shape=(
            jax.ShapeDtypeStruct((6, nrows, LANES), f32),
            jax.ShapeDtypeStruct((6, cz, cy), f32),
            jax.ShapeDtypeStruct((nrows, LANES), f32),
            jax.ShapeDtypeStruct((cz, cy), f32),
        ),
        in_specs=[vm] * 9,
        out_specs=(vm,) * 4,
        scratch_shapes=[
            pltpu.VMEM((STEPS + 1, 2, 6, fz, fy), f32),
            pltpu.VMEM((STEPS, 6, rows_c, cy), f32),
            pltpu.VMEM((STEPS, 2, 6, fz, fy), f32),
            pltpu.VMEM((STEPS, 2, 6, rows_c, cy), f32),
            pltpu.VMEM((STEPS, 2, split, LANES), f32),
            pltpu.VMEM((STEPS, 2, split, LANES), f32),
            pltpu.VMEM((STEPS, 2, split, LANES), f32),
            pltpu.VMEM((STEPS, split, LANES), f32),
            pltpu.VMEM((8, fy), f32),
            pltpu.VMEM((2, 8, fy), f32),
            pltpu.VMEM((4, 3, fz + 16, fy + LANES), f32),
            pltpu.VMEM((3, 3, cz + 16, cy + LANES), f32),
            pltpu.VMEM((16, max(fy, cy + LANES)), f32),
            pltpu.VMEM((16, fy + LANES), f32),
            dma((STEPS, 2, 2, 2)),
            dma((STEPS, 2, 2, 2)),
            dma((STEPS, 2)),
            dma((STEPS, 2)),
            dma((STEPS, 2)),
            dma((STEPS, 2)),
            dma((2,)),
            dma((2,)),
        ],
        compiler_params=pltpu.CompilerParams(collective_id=0, has_side_effects=True),
        name="wave",
    )(
        rows_view(fold),
        rows_view(fnow),
        cold.reshape(6, cz, cy),
        cnow.reshape(6, cz, cy),
        rows_view(shf),
        rows_view(laf),
        shc.reshape(cz, cy),
        lac.reshape(cz, cy),
        topo,
    )
    return (
        rows_back(fout, fold.shape),
        cout.reshape(cold.shape),
        rows_back(fker, shf.shape),
        cker.reshape(shc.shape),
    )


def solution(mesh):
    field, coef = P(None, None, None, "gx", "gy"), P(None, "gx", "gy")
    return jax.shard_map(
        on_device,
        mesh=mesh,
        in_specs=(field,) * 4 + (coef,) * 4 + (P("gx", "gy"),),
        out_specs=(field, field, coef, coef),
        check_vma=False,
    )
```
